512 devices in a mesh: serve: 32 (over z_hi, x, core), tensor: 16 (over z_lo, y).
Axes of the slice: x: 4, y: 8, z: 8 (z_hi: 4, z_lo: 2; z = z_hi * 2 + z_lo), core: 2. Of those that a mesh axis runs over, the one named last changes fastest.
Arguments:
- queries: bfloat16 [32768, 4096], P('serve', 'tensor'), may hold values from -8 to 8
- kv_cache: bfloat16 [32, 6400, 256], P('serve', 'tensor'), may hold values from -6 to 6
- question_slot: int32 [1024], P('serve'), may hold values from 0 to 3, as said below
- question_len: int32 [1024], P('serve'), may hold values from 1 to 32, 20480 in all
- out_weight: bfloat16 [4096, 8192], P(None, 'tensor'), may hold values from -0.375 to 0.375
Outputs:
- answers: bfloat16 [32768, 8192], P('serve', 'tensor')
The draws below stay inside these ranges and needn't reach their ends.
Inputs may be any that keep to these rules, and one draw needn't show every extreme that they name: Question q of serving group g asks about the image held by serving group (g - question_slot[q]) mod 32; among one serving group's 32 questions every value 0 to 3 occurs exactly 32 / 4 times.
All inputs are finite; a program needn't handle non-finite values. No bound on the sum of `question_len` on one device may be relied on, other than what follows from the above.
Results may differ from the reference program's by a relative error of at most 0.0058.
Values may be sent and summed in bfloat16 or wider, within the bound.
A program may use at most 64 MiB of HBM per device.

```python
import math
import jax
import jax.numpy as jnp
import numpy as np
from jax import lax

D = 8192
HEADS = 32
KVH = 4
HEAD_DIM = 128
P_SIZE = 1600
Q_GRP = 32
QLEN = 32
NEED = 4
IMAGES = 32
QUESTIONS = 1024
ROWS = 32768
N_SERVE = 32


def slot_values(key):
    group_keys = jax.random.split(jax.random.fold_in(key, 17), IMAGES)
    base_slots = (jnp.arange(Q_GRP, dtype=jnp.int32) % NEED).astype(jnp.int32)
    shuffled = jax.vmap(lambda one_key: jax.random.permutation(one_key, base_slots))(group_keys)
    return shuffled.reshape(QUESTIONS).astype(jnp.int32)


def draw_question_slot(key, part):
    return slot_values(key)


def draw_queries(key, part):
    base = 2.0 * jax.random.normal(jax.random.fold_in(key, 23), (ROWS, HEADS * HEAD_DIM), jnp.float32)
    base = jnp.clip(base, -8.0, 8.0)
    return base.astype(jnp.bfloat16)


def draw_kv_cache(key, part):
    base = jax.random.normal(jax.random.fold_in(key, 29), (IMAGES, KVH, P_SIZE, 2 * HEAD_DIM), jnp.float32)
    base = jnp.clip(base, -6.0, 6.0)
    return base.reshape(IMAGES, KVH * P_SIZE, 2 * HEAD_DIM).astype(jnp.bfloat16)


def block_scale(rng, dims, shards, low, top_value):
    level = 1.0
    for dim, parts in shards:
        draws = jax.random.uniform(jax.random.fold_in(jax.random.fold_in(rng, 6), dim), (parts,), jnp.float32, low / len(shards), top_value / len(shards))
        level = level * jnp.repeat(jnp.exp(draws), dims[dim] // parts).reshape((-1,) + (1,) * (len(dims) - 1 - dim))
    return level


def profile(amount, total, limit, skew):
    portions = [(1 << 20) // math.isqrt(standing ** skew) + 1 for standing in range(2, amount + 1)]
    spare, counts = total - limit - (amount - 1), [1] * (amount - 1)
    while spare > 0:
        movable = [i for i in range(amount - 1) if counts[i] < limit]
        pool, budget = sum([portions[i] for i in movable]), spare
        for i in movable:
            addition = min(limit - counts[i], max(1, budget * portions[i] // pool), spare)
            counts[i] = counts[i] + addition
            spare = spare - addition
    return np.array([limit] + counts)


def ragged_sizes(stream_key, count, total, most, lean):
    if count == 2:
        one = jax.random.randint(stream_key, (), max(1, total - most), min(most, total - 1) + 1)
        return jnp.stack([one, total - one])
    lengths = jnp.asarray(profile(count, total, most, lean), jnp.int32)
    twos = (count - 1) // 2
    source_of, taker = lengths[1:1 + 2 * twos:2], lengths[2:2 + 2 * twos:2]
    room = jnp.minimum(source_of - 1, most - taker)
    shifted = jax.random.randint(jax.random.fold_in(stream_key, 1), (twos,), 0, 1 << 20) % (room + 1)
    lengths = lengths.at[1:1 + 2 * twos:2].set(source_of - shifted).at[2:2 + 2 * twos:2].set(taker + shifted)
    return lengths[jax.random.permutation(jax.random.fold_in(stream_key, 2), count)]


def bell_draw(own_key, extent, width, limit, cuts=(), kind=jnp.bfloat16):
    values = jax.random.normal(own_key, extent, jnp.float32) * width
    if len(cuts) > 0:
        values = block_scale(own_key, extent, cuts, -0.22, 0.18) * values
    return jnp.clip(values, min=-limit, max=limit).astype(kind)


def setup_inputs(seed: int = 0) -> dict:
    arg_keys = jax.random.split(jax.random.key(seed), 6)
    queries = draw_queries(jax.random.fold_in(arg_keys[5], 71), 0)
    kv_cache = draw_kv_cache(jax.random.fold_in(arg_keys[5], 71), 0)
    question_slot = draw_question_slot(jax.random.fold_in(arg_keys[5], 71), 0)
    question_len = ragged_sizes(arg_keys[3], QUESTIONS, QUESTIONS * QLEN * 5 // 8, QLEN, 2).astype(jnp.int32)
    out_weight = bell_draw(arg_keys[4], (HEADS * HEAD_DIM, D), (HEADS * HEAD_DIM // 16) ** -0.5, 0.375, ((1, 16),))
    return {"queries": queries, "kv_cache": kv_cache, "question_slot": question_slot, "question_len": question_len, "out_weight": out_weight}


def attend_one(query_rows, key_value):
    head_dim = key_value.shape[2] // 2
    grouped = query_rows.reshape(query_rows.shape[0], key_value.shape[0], -1, head_dim)
    key_part = key_value[:, :, :head_dim]
    value_part = key_value[:, :, head_dim:]
    scores = jnp.einsum("rkgd,kpd->kgrp", grouped, key_part, precision=lax.Precision.HIGHEST) * (head_dim ** -0.5)
    row_max = jnp.max(scores, axis=3, keepdims=True)
    exp_scores = jnp.exp(scores - row_max)
    sum_exp = jnp.sum(exp_scores, axis=3, keepdims=True)
    weights = lax.optimization_barrier((exp_scores / sum_exp).astype(jnp.bfloat16)).astype(jnp.float32)
    blended = jnp.einsum("kgrp,kpd->rkgd", weights, value_part, precision=lax.Precision.HIGHEST)
    return blended.reshape(query_rows.shape[0], -1)


def reference(queries, kv_cache, question_slot, question_len, out_weight):
    row_count = queries.shape[0]
    question_count = row_count // QLEN
    owner_group = (jnp.arange(question_count, dtype=jnp.int32) // Q_GRP - question_slot) % N_SERVE
    owner_group = owner_group.astype(jnp.int32)
    per_question = queries.reshape(question_count, QLEN, queries.shape[1])

    def one_question(packed):
        query_rows, image_index, length = packed
        key_value = lax.dynamic_index_in_dim(kv_cache, image_index, 0, keepdims=False)
        key_value = key_value.reshape(KVH, -1, key_value.shape[1]).astype(jnp.float32)
        blended = attend_one(query_rows.astype(jnp.float32), key_value)
        live_rows = jnp.arange(QLEN, dtype=jnp.int32) < length
        return jnp.where(live_rows[:, None], blended, jnp.float32(0.0)).astype(jnp.bfloat16)

    attended = lax.map(one_question, (per_question, owner_group, question_len))
    attended = attended.reshape(row_count, queries.shape[1])
    return jnp.dot(attended, out_weight, preferred_element_type=jnp.float32).astype(jnp.bfloat16)
```

```python
import functools

import jax
import jax.numpy as jnp
from jax import lax
from jax.experimental import pallas as pl
from jax.experimental.pallas import tpu as pltpu
from jax.sharding import PartitionSpec as P

QLEN = 32
NEED = 4
RING = 8
SHARE = 4
HEAD_DIM = 128
SUBS = 2
MESH = pl.DeviceIdType.MESH
F32 = jnp.float32
BF16 = jnp.bfloat16


def event_order(chunks):
    events = [(3.5 * c + 3 * k, c, k) for c in range(chunks) for k in range(5)]
    return [(c, k) for _, c, k in sorted(events)]


def kernel(n_serve, q_hbm, kv_hbm, len_ref, w_hbm, out_hbm,
           sq, vq, ao, kvb, g, wo, wp, acc, ps, pr, ob,
           local_sem, ob_sem, kv_sr, kv_rr, kv_sl, kv_rl, q_s, q_r, ret_s, ret_r,
           w_s, w_r, wf_s, wf_r, ag_sr, ag_rr, ag_sl, ag_rl, p_s, p_r):
    s = lax.axis_index("serve")
    t = lax.axis_index("tensor")
    y = lax.rem(t, RING)
    z = t // RING
    p = lax.rem(t, SHARE)
    core = lax.rem(s, 2)
    right = (s, z * RING + lax.rem(y + 1, RING))
    left = (s, z * RING + lax.rem(y + RING - 1, RING))
    mate = (s, lax.rem(t + RING, 2 * RING))
    sibling = (s + 1 - 2 * core, t)
    owner = [None] + [(lax.rem(s + n_serve - j, n_serve), t) for j in range(1, NEED)]
    asker = [None] + [(lax.rem(s + j, n_serve), t) for j in range(1, NEED)]

    rows, cols = q_hbm.shape
    slot_rows = rows // NEED
    chunks = NEED * SUBS
    sub = slot_rows // SUBS
    piece = kv_hbm.shape[0]
    half = wo.shape[0]
    out_cols = wo.shape[1]
    wpart = half // 4
    scale = HEAD_DIM ** -0.5

    def remote(src, dst, send, recv, device):
        return pltpu.make_async_remote_copy(
            src_ref=src, dst_ref=dst, send_sem=send, recv_sem=recv,
            device_id=device, device_id_type=MESH)

    barrier = pltpu.get_barrier_semaphore()
    partners = [owner[3], asker[3], owner[2], asker[2], owner[1], asker[1], mate, right, left]
    for device in partners:
        pl.semaphore_signal(barrier, inc=1, device_id=device, device_id_type=MESH)

    q_load = pltpu.make_async_copy(q_hbm.at[pl.ds(0, slot_rows), :], sq, local_sem.at[0])
    q_load.start()

    def kv_rows(index):
        return kvb.at[pl.ds(pl.multiple_of(index * piece, 16), piece), :]

    kv_load = pltpu.make_async_copy(kv_hbm, kv_rows(p), local_sem.at[1])
    kv_load.start()
    w_load = pltpu.make_async_copy(
        w_hbm.at[pl.ds(pl.multiple_of(z * half, half), half), :], wo, local_sem.at[2])
    w_load.start()

    pl.semaphore_wait(barrier, len(partners))

    def kv_right(k):
        src = kv_hbm if k == 0 else kv_rows(p - k)
        return remote(src, kv_rows(p - k), kv_sr.at[k], kv_rr.at[k], right)

    def kv_left(k):
        src = kv_hbm if k == 0 else kv_rows(p + k)
        return remote(src, kv_rows(p + k), kv_sl.at[k], kv_rl.at[k], left)

    def kv_from_left(k):
        dst = kv_rows(p - k)
        return remote(dst, dst, kv_sr.at[k - 1], kv_rr.at[k - 1], left)

    def kv_from_right(k):
        dst = kv_rows(p + k)
        return remote(dst, dst, kv_sl.at[k - 1], kv_rl.at[k - 1], right)

    @pl.when(p < SHARE - 1)
    def _():
        kv_right(0).start()

    @pl.when(p > 0)
    def _():
        kv_left(0).start()

    def kv_step(k):
        @pl.when(p >= k)
        def _():
            kv_from_left(k).wait_recv()
            if k < SHARE - 1:
                @pl.when(p < SHARE - 1)
                def _():
                    kv_right(k).start()

        @pl.when(p + k < SHARE)
        def _():
            kv_from_right(k).wait_recv()
            if k < SHARE - 1:
                @pl.when(p > 0)
                def _():
                    kv_left(k).start()

    def ask(j, b):
        first = j * slot_rows + b * sub
        return remote(q_hbm.at[pl.ds(first, sub), :], vq.at[j - 1, pl.ds(b * sub, sub), :],
                      q_s.at[j - 1, b], q_r.at[j - 1, b], owner[j])

    for j in range(1, NEED):
        for b in range(SUBS):
            ask(j, b).start()

    def w_out(i):
        first = (1 - z) * half + core * (2 * wpart) + i * wpart
        return remote(w_hbm.at[pl.ds(pl.multiple_of(first, wpart), wpart), :],
                      wp.at[pl.ds(pl.multiple_of(core * (2 * wpart) + i * wpart, wpart), wpart), :],
                      w_s.at[i], w_r.at[i], mate)

    def w_swap(i):
        part = wp.at[pl.ds(pl.multiple_of(core * (2 * wpart) + i * wpart, wpart), wpart), :]
        return remote(part, part, wf_s.at[i], wf_r.at[i], sibling)

    def w_swapped(i):
        part = wp.at[pl.ds(pl.multiple_of((1 - core) * (2 * wpart) + i * wpart, wpart), wpart), :]
        return remote(part, part, wf_s.at[i], wf_r.at[i], sibling)

    for i in range(2):
        w_out(i).start()
    q_load.wait()
    kv_step(1)
    kv_step(2)
    kv_step(3)
    kv_load.wait()

    def attend(q_ref, o_ref):
        for h in range(cols // HEAD_DIM):
            query = q_ref[:, h * HEAD_DIM:(h + 1) * HEAD_DIM]
            scores = lax.dot_general(query, kvb[:, :HEAD_DIM], (((1,), (1,)), ((), ())),
                                     preferred_element_type=F32)
            top = jnp.max(scores, axis=1, keepdims=True)
            exps = jnp.exp((scores - top) * scale)
            total = jnp.sum(exps, axis=1, keepdims=True)
            blend = jnp.dot(exps.astype(BF16), kvb[:, HEAD_DIM:], preferred_element_type=F32)
            o_ref[:, h * HEAD_DIM:(h + 1) * HEAD_DIM] = (blend / total).astype(BF16)

    reach_right = [4 if c % 2 == 0 else 3 for c in range(chunks)]
    reach_left = [3 if c % 2 == 0 else 4 for c in range(chunks)]

    def block(origin, c):
        return g.at[lax.rem(origin + RING, RING), pl.ds(c * sub, sub), :]

    def go_right(c, k):
        part = block(y - k, c)
        return remote(part, part, ag_sr.at[c, k], ag_rr.at[c, k], right)

    def go_left(c, k):
        part = block(y + k, c)
        return remote(part, part, ag_sl.at[c, k], ag_rl.at[c, k], left)

    def from_left(c, k):
        part = block(y - k, c)
        return remote(part, part, ag_sr.at[c, k - 1], ag_rr.at[c, k - 1], left)

    def from_right(c, k):
        part = block(y + k, c)
        return remote(part, part, ag_sl.at[c, k - 1], ag_rl.at[c, k - 1], right)

    def answer(j, b):
        c = j * SUBS + b
        return remote(ao.at[j - 1, pl.ds(b * sub, sub), :], block(y, c),
                      ret_s.at[j - 1, b], ret_r.at[j - 1, b], asker[j])

    def answered(j, b):
        part = block(y, j * SUBS + b)
        return remote(part, part, ret_s.at[j - 1, b], ret_r.at[j - 1, b], owner[j])

    def visit(j, b):
        spot = pl.ds(b * sub, sub)
        remote(vq.at[j - 1, spot, :], vq.at[j - 1, spot, :],
               q_s.at[j - 1, b], q_r.at[j - 1, b], asker[j]).wait_recv()
        attend(vq.at[j - 1, spot, :], ao.at[j - 1, spot, :])
        answer(j, b).start()

    def partial(c):
        return remote(ps.at[c], pr.at[c], p_s.at[c], p_r.at[c], mate)

    def project(c):
        lhs = jnp.concatenate([g[i, c * sub:(c + 1) * sub, :] for i in range(RING)], axis=1)
        ps[c] = jnp.dot(lhs, wp[...], preferred_element_type=F32).astype(BF16)
        partial(c).start()
        acc[c * sub:(c + 1) * sub, :] = jnp.dot(lhs, wo[...], preferred_element_type=F32)

    def write(c):
        part = pl.ds(c * sub, sub)
        return pltpu.make_async_copy(ob.at[part, :], out_hbm.at[part, :], ob_sem.at[c])

    def finish(c):
        partial(c).wait_recv()
        token = lax.broadcasted_iota(jnp.int32, (QLEN, out_cols), 0)
        for i in range(sub // QLEN):
            part = slice(c * sub + i * QLEN, c * sub + (i + 1) * QLEN)
            total = acc[part, :] + pr[c, i * QLEN:(i + 1) * QLEN, :].astype(F32)
            live = token < len_ref[c * (sub // QLEN) + i]
            ob[part, :] = jnp.where(live, total, 0.0).astype(BF16)
        write(c).start()

    done = set()

    def event(c, k):
        if (c, k) in done:
            return
        done.add((c, k))
        if k == 0:
            if c < SUBS:
                attend(sq.at[pl.ds(c * sub, sub), :], g.at[y, pl.ds(c * sub, sub), :])
            else:
                answered(c // SUBS, c % SUBS).wait_recv()
            go_right(c, 0).start()
            go_left(c, 0).start()
            return
        if k <= reach_right[c]:
            from_left(c, k).wait_recv()
            if k < reach_right[c]:
                go_right(c, k).start()
        if k <= reach_left[c]:
            from_right(c, k).wait_recv()
            if k < reach_left[c]:
                go_left(c, k).start()
        if k == 4:
            if c == 0:
                w_load.wait()
                for i in range(2):
                    w_swapped(i).wait_recv()
            project(c)
            if c >= 1:
                finish(c - 1)

    def w_relay(i):
        w_out(i).wait_recv()
        w_swap(i).start()

    event(0, 0)
    event(1, 0)
    visit(1, 0)
    visit(1, 1)
    event(0, 1)
    event(1, 1)
    visit(2, 0)
    visit(2, 1)
    event(0, 2)
    event(1, 2)
    event(2, 0)
    visit(3, 0)
    event(3, 0)
    visit(3, 1)
    w_relay(0)
    event(0, 3)
    event(1, 3)
    event(2, 1)
    event(3, 1)
    w_relay(1)
    for c, k in event_order(chunks):
        event(c, k)
    finish(chunks - 1)

    for k in range(SHARE - 1):
        @pl.when(jnp.logical_and(p >= k, p < SHARE - 1))
        def _(k=k):
            kv_right(k).wait_send()

        @pl.when(jnp.logical_and(p + k < SHARE, p > 0))
        def _(k=k):
            kv_left(k).wait_send()
    for j in range(1, NEED):
        for b in range(SUBS):
            ask(j, b).wait_send()
            answer(j, b).wait_send()
    for i in range(2):
        w_out(i).wait_send()
        w_swap(i).wait_send()
    for c in range(chunks):
        for k in range(reach_right[c]):
            go_right(c, k).wait_send()
        for k in range(reach_left[c]):
            go_left(c, k).wait_send()
        partial(c).wait_send()
        write(c).wait()


def on_device(queries, kv_cache, question_slot, question_len, out_weight):
    rows, cols = queries.shape
    piece, width = kv_cache.shape[1:]
    depth, out_cols = out_weight.shape
    questions = rows // QLEN
    chunks = NEED * SUBS
    sub = rows // chunks
    slot_rows = rows // NEED
    dma = pltpu.SemaphoreType.DMA
    index = jnp.arange(questions, dtype=jnp.int32)
    same = question_slot[:, None] == question_slot[None, :]
    earlier = jnp.sum(jnp.where(same & (index[None, :] < index[:, None]), 1, 0), axis=1)
    pos = question_slot * (questions // NEED) + earlier
    chosen = pos[None, :] == index[:, None]
    order = jnp.sum(jnp.where(chosen, index[None, :], 0), axis=1)
    lengths = jnp.sum(jnp.where(chosen, question_len[None, :], 0), axis=1)
    sorted_rows = queries.reshape(questions, QLEN, cols)[order].reshape(rows, cols)
    ordered = pl.pallas_call(
        functools.partial(kernel, lax.axis_size("serve")),
        out_shape=jax.ShapeDtypeStruct((rows, out_cols), BF16),
        in_specs=[
            pl.BlockSpec(memory_space=pl.ANY),
            pl.BlockSpec(memory_space=pl.ANY),
            pl.BlockSpec(memory_space=pltpu.SMEM),
            pl.BlockSpec(memory_space=pl.ANY),
        ],
        out_specs=pl.BlockSpec(memory_space=pl.ANY),
        scratch_shapes=[
            pltpu.VMEM((slot_rows, cols), BF16),
            pltpu.VMEM((NEED - 1, slot_rows, cols), BF16),
            pltpu.VMEM((NEED - 1, slot_rows, cols), BF16),
            pltpu.VMEM((SHARE * piece, width), BF16),
            pltpu.VMEM((RING, rows, cols), BF16),
            pltpu.VMEM((depth // 2, out_cols), BF16),
            pltpu.VMEM((depth // 2, out_cols), BF16),
            pltpu.VMEM((rows, out_cols), F32),
            pltpu.VMEM((chunks, sub, out_cols), BF16),
            pltpu.VMEM((chunks, sub, out_cols), BF16),
            pltpu.VMEM((rows, out_cols), BF16),
            dma((3,)), dma((chunks,)),
            dma((3,)), dma((3,)), dma((3,)), dma((3,)),
            dma((NEED - 1, SUBS)), dma((NEED - 1, SUBS)), dma((NEED - 1, SUBS)), dma((NEED - 1, SUBS)),
            dma((2,)), dma((2,)), dma((2,)), dma((2,)),
            dma((chunks, 4)), dma((chunks, 4)), dma((chunks, 4)), dma((chunks, 4)),
            dma((chunks,)), dma((chunks,)),
        ],
        compiler_params=pltpu.CompilerParams(
            collective_id=0, has_side_effects=True, vmem_limit_bytes=56 * 1024 * 1024),
    )(sorted_rows, kv_cache.reshape(piece, width), lengths, out_weight)
    return ordered.reshape(questions, QLEN, out_cols)[pos].reshape(rows, out_cols)


def solution(mesh):
    return jax.shard_map(
        on_device,
        mesh=mesh,
        in_specs=(
            P("serve", "tensor"),
            P("serve", "tensor", None),
            P("serve"),
            P("serve"),
            P(None, "tensor"),
        ),
        out_specs=P("serve", "tensor"),
        check_vma=False,
    )
```

```python
import functools

import jax
import jax.numpy as jnp
from jax import lax
from jax.experimental import pallas as pl
from jax.experimental.pallas import tpu as pltpu
from jax.sharding import PartitionSpec as P

QLEN = 32
NEED = 4
RING = 8
SHARE = 4
HEAD_DIM = 128
MESH = pl.DeviceIdType.MESH
F32 = jnp.float32
BF16 = jnp.bfloat16
VMEM_LIMIT = 56 * 1024 * 1024


def remote(src, dst, send, recv, device):
    return pltpu.make_async_remote_copy(
        src_ref=src, dst_ref=dst, send_sem=send, recv_sem=recv,
        device_id=device, device_id_type=MESH)


def greet(partners):
    barrier = pltpu.get_barrier_semaphore()
    for device in partners:
        pl.semaphore_signal(barrier, inc=1, device_id=device, device_id_type=MESH)
    return lambda: pl.semaphore_wait(barrier, len(partners))


def attend(q_ref, kvb, o_ref):
    for h in range(q_ref.shape[1] // HEAD_DIM):
        query = q_ref[:, h * HEAD_DIM:(h + 1) * HEAD_DIM]
        scores = lax.dot_general(query, kvb[:, :HEAD_DIM], (((1,), (1,)), ((), ())),
                                 preferred_element_type=F32)
        top = jnp.max(scores, axis=1, keepdims=True)
        exps = jnp.exp((scores - top) * HEAD_DIM ** -0.5)
        total = jnp.sum(exps, axis=1, keepdims=True)
        blend = jnp.dot(exps.astype(BF16), kvb[:, HEAD_DIM:], preferred_element_type=F32)
        o_ref[:, h * HEAD_DIM:(h + 1) * HEAD_DIM] = (blend / total).astype(BF16)


def chunk_list(rows):
    sub = rows // (2 * NEED)
    chunks = [(i * sub, sub, i // 2) for i in range(2 * NEED - 1)]
    return chunks + [(rows - sub, sub // 2, NEED - 1), (rows - sub // 2, sub // 2, NEED - 1)]


def exchange(n_serve, chunks, q_hbm, kv_hbm, slot_ref, len_ref, w_hbm, out_hbm, place_out,
             qv, sq, vq, ao, kvb, g, wo, wp, acc, ps, pr, ob, live_ref,
             local_sem, ob_sem, kv_sr, kv_rr, kv_sl, kv_rl, q_s, q_r, ret_s, ret_r,
             w_s, w_r, wf_s, wf_r, ag_sr, ag_rr, ag_sl, ag_rl, p_s, p_r):
    s = lax.axis_index("serve")
    t = lax.axis_index("tensor")
    y = lax.rem(t, RING)
    z = t // RING
    p = lax.rem(t, SHARE)
    core = lax.rem(s, 2)
    right = (s, z * RING + lax.rem(y + 1, RING))
    left = (s, z * RING + lax.rem(y + RING - 1, RING))
    mate = (s, lax.rem(t + RING, 2 * RING))
    sibling = (s + 1 - 2 * core, t)
    owner = [None] + [(lax.rem(s + n_serve - j, n_serve), t) for j in range(1, NEED)]
    asker = [None] + [(lax.rem(s + j, n_serve), t) for j in range(1, NEED)]
    rows, cols = q_hbm.shape
    questions = rows // QLEN
    slot_rows = rows // NEED
    piece = kv_hbm.shape[0]
    half, out_cols = wo.shape
    wpart = half // 4

    wait_entry = greet([owner[3], asker[3], owner[2], asker[2], owner[1], asker[1], mate, right, left])
    q_load = pltpu.make_async_copy(q_hbm, qv, local_sem.at[0])
    q_load.start()

    def kv_rows(index):
        return kvb.at[pl.ds(pl.multiple_of(index * piece, 16), piece), :]

    kv_load = pltpu.make_async_copy(kv_hbm, kv_rows(p), local_sem.at[1])
    kv_load.start()
    w_load = pltpu.make_async_copy(
        w_hbm.at[pl.ds(pl.multiple_of(z * half, half), half), :], wo, local_sem.at[2])
    w_load.start()
    wait_entry()

    def kv_right(k):
        src = kv_hbm if k == 0 else kv_rows(p - k)
        return remote(src, kv_rows(p - k), kv_sr.at[k], kv_rr.at[k], right)

    def kv_left(k):
        src = kv_hbm if k == 0 else kv_rows(p + k)
        return remote(src, kv_rows(p + k), kv_sl.at[k], kv_rl.at[k], left)

    @pl.when(p < SHARE - 1)
    def _():
        kv_right(0).start()

    @pl.when(p > 0)
    def _():
        kv_left(0).start()

    def kv_step(k):
        @pl.when(p >= k)
        def _():
            dst = kv_rows(p - k)
            remote(dst, dst, kv_sr.at[k - 1], kv_rr.at[k - 1], left).wait_recv()
            if k < SHARE - 1:
                @pl.when(p < SHARE - 1)
                def _():
                    kv_right(k).start()

        @pl.when(p + k < SHARE)
        def _():
            dst = kv_rows(p + k)
            remote(dst, dst, kv_sl.at[k - 1], kv_rl.at[k - 1], right).wait_recv()
            if k < SHARE - 1:
                @pl.when(p > 0)
                def _():
                    kv_left(k).start()

    slot = slot_ref[...]
    mine = (lax.broadcasted_iota(jnp.int32, (8, questions), 0) == slot).astype(F32)
    before = (lax.broadcasted_iota(jnp.int32, (questions, questions), 0)
              < lax.broadcasted_iota(jnp.int32, (questions, questions), 1)).astype(F32)
    rank = jnp.dot(mine.astype(BF16), before.astype(BF16), preferred_element_type=F32)
    place = jnp.sum(mine * rank, axis=0, keepdims=True) + slot.astype(F32) * (questions // NEED)
    spread = (lax.broadcasted_iota(jnp.int32, (questions, rows), 1) // QLEN
              == lax.broadcasted_iota(jnp.int32, (questions, rows), 0)).astype(BF16)
    both = jnp.concatenate([place, len_ref[...].astype(F32), jnp.zeros((6, questions), F32)], axis=0)
    both = jnp.dot(both.astype(BF16), spread, preferred_element_type=F32).astype(jnp.int32)
    token = lax.broadcasted_iota(jnp.int32, (1, rows), 1) % QLEN
    row = both[0:1, :] * QLEN + token
    live = (token < both[1:2, :]).astype(F32)
    place_out[...] = place.astype(jnp.int32)

    q_load.wait()

    def sort(j):
        first = j * slot_rows
        chosen = (lax.broadcasted_iota(jnp.int32, (slot_rows, rows), 0) + first == row).astype(F32)
        sq[pl.ds(first, slot_rows), :] = jnp.dot(
            chosen.astype(BF16), qv[...], preferred_element_type=F32).astype(BF16)
        live_ref[pl.ds(first, slot_rows), :] = jnp.sum(chosen * live, axis=1, keepdims=True)

    def spot(c):
        first, size, _ = chunks[c]
        return pl.ds(first - slot_rows, size)

    def part_of(ref, c):
        first, size, _ = chunks[c]
        return ref.at[pl.ds(first, size), :]

    def ask(c):
        return remote(part_of(sq, c), vq.at[spot(c), :], q_s.at[c], q_r.at[c], owner[chunks[c][2]])

    def w_part(side, i):
        return wp.at[pl.ds(pl.multiple_of(side * (2 * wpart) + i * wpart, wpart), wpart), :]

    def w_out(i):
        first = (1 - z) * half + core * (2 * wpart) + i * wpart
        return remote(w_hbm.at[pl.ds(pl.multiple_of(first, wpart), wpart), :], w_part(core, i),
                      w_s.at[i], w_r.at[i], mate)

    def w_swap(i):
        return remote(w_part(core, i), w_part(core, i), wf_s.at[i], wf_r.at[i], sibling)

    def w_relay(i):
        w_out(i).wait_recv()
        w_swap(i).start()

    def w_ready():
        w_load.wait()
        for i in range(2):
            part = w_part(1 - core, i)
            remote(part, part, wf_s.at[i], wf_r.at[i], sibling).wait_recv()

    count = len(chunks)
    visitors = [c for c in range(count) if chunks[c][2] > 0]
    for j in range(1, NEED):
        sort(j)
        for c in visitors:
            if chunks[c][2] == j:
                ask(c).start()
    w_out(0).start()
    w_out(1).start()
    kv_step(1)
    sort(0)
    kv_step(2)
    kv_step(3)
    kv_load.wait()

    reach_right = [4 if c % 2 == 0 else 3 for c in range(len(chunks))]
    reach_left = [3 if c % 2 == 0 else 4 for c in range(len(chunks))]

    def block(origin, c):
        first, size, _ = chunks[c]
        return g.at[lax.rem(origin + RING, RING), pl.ds(first, size), :]

    def go_right(c, k):
        return remote(block(y - k, c), block(y - k, c),
                      ag_sr.at[c, k], ag_rr.at[c, k], right)

    def go_left(c, k):
        return remote(block(y + k, c), block(y + k, c),
                      ag_sl.at[c, k], ag_rl.at[c, k], left)

    def from_left(c, k):
        part = block(y - k, c)
        return remote(part, part, ag_sr.at[c, k - 1], ag_rr.at[c, k - 1], left)

    def from_right(c, k):
        part = block(y + k, c)
        return remote(part, part, ag_sl.at[c, k - 1], ag_rl.at[c, k - 1], right)

    def answer(c):
        return remote(ao.at[spot(c), :], block(y, c), ret_s.at[c], ret_r.at[c], asker[chunks[c][2]])

    def visit(c):
        slot = chunks[c][2]
        remote(vq.at[spot(c), :], vq.at[spot(c), :], q_s.at[c], q_r.at[c], asker[slot]).wait_recv()
        attend(vq.at[spot(c), :], kvb, ao.at[spot(c), :])
        answer(c).start()

    def partial(c):
        return remote(part_of(ps, c), part_of(pr, c), p_s.at[c], p_r.at[c], mate)

    def project(c):
        first, size, slot = chunks[c]
        lhs = jnp.concatenate([g[i, first:first + size, :] for i in range(RING)], axis=1)
        ps[first:first + size, :] = jnp.dot(lhs, wp[...], preferred_element_type=F32).astype(BF16)
        partial(c).start()
        acc[first:first + size, :] = jnp.dot(lhs, wo[...], preferred_element_type=F32)

    def write(c):
        return pltpu.make_async_copy(part_of(ob, c), part_of(out_hbm, c), ob_sem.at[c])

    def finish(c):
        first, size, _ = chunks[c]
        partial(c).wait_recv()
        part = slice(first, first + size)
        total = acc[part, :] + pr[part, :].astype(F32)
        ob[part, :] = jnp.where(live_ref[part, :] > 0.5, total, 0.0).astype(BF16)
        write(c).start()

    def start(c):
        if chunks[c][2] > 0:
            part = block(y, c)
            remote(part, part, ret_s.at[c], ret_r.at[c], owner[chunks[c][2]]).wait_recv()
        else:
            attend(part_of(sq, c), kvb, block(y, c))
        go_right(c, 0).start()
        go_left(c, 0).start()

    def step(c, k):
        if k <= reach_right[c]:
            from_left(c, k).wait_recv()
            if k < reach_right[c]:
                go_right(c, k).start()
        if k <= reach_left[c]:
            from_right(c, k).wait_recv()
            if k < reach_left[c]:
                go_left(c, k).start()

    tasks = []
    ready = {}
    for c, (first, size, slot) in enumerate(chunks):
        begin = 3.5 * first
        if slot > 0:
            tasks.append((begin, functools.partial(start, c)))
        for k in range(1, 5):
            tasks.append((begin + LAG * k * max(size, 96), functools.partial(step, c, k)))
        ready[c] = max(begin + LAG * 4 * max(size, 96) + 1, W_TIME + 2 + c)
        tasks.append((ready[c], functools.partial(project, c)))
        tasks.append((ready[c] + 450 if c < count - 1 else 1e9, functools.partial(finish, c)))
    for i, c in enumerate(visitors):
        tasks.append((VISIT[chunks[c][2]] + i, functools.partial(visit, c)))
    tasks.append((15, functools.partial(w_relay, 0)))
    tasks.append((W_TIME, functools.partial(w_relay, 1)))
    tasks.append((W_TIME + 1, w_ready))
    tasks.sort(key=lambda task: task[0])
    start(0)
    start(1)
    for _, task in tasks:
        task()

    for k in range(SHARE - 1):
        @pl.when(jnp.logical_and(p >= k, p < SHARE - 1))
        def _(k=k):
            kv_right(k).wait_send()

        @pl.when(jnp.logical_and(p + k < SHARE, p > 0))
        def _(k=k):
            kv_left(k).wait_send()
    for c in visitors:
        ask(c).wait_send()
        answer(c).wait_send()
    for i in range(2):
        w_out(i).wait_send()
        w_swap(i).wait_send()
    for c in range(count):
        for k in range(reach_right[c]):
            go_right(c, k).wait_send()
        for k in range(reach_left[c]):
            go_left(c, k).wait_send()
        partial(c).wait_send()
        write(c).wait()


LAG = 2.2
W_TIME = 900
VISIT = [0, 10, 310, 620]


def unsort(place_ref, ordered, out, held, in_sem, out_sem):
    questions = place_ref.shape[0]

    def fetch(q):
        return pltpu.make_async_copy(
            ordered.at[pl.ds(pl.multiple_of(place_ref[q] * QLEN, QLEN), QLEN), :],
            held.at[pl.ds(q * QLEN, QLEN), :], in_sem.at[q])

    def store(q):
        part = pl.ds(q * QLEN, QLEN)
        return pltpu.make_async_copy(held.at[part, :], out.at[part, :], out_sem.at[q])

    for q in range(questions):
        fetch(q).start()
    for q in range(questions):
        fetch(q).wait()
        store(q).start()
    for q in range(questions):
        store(q).wait()


def on_device(queries, kv_cache, question_slot, question_len, out_weight):
    rows, cols = queries.shape
    piece, width = kv_cache.shape[1:]
    depth, out_cols = out_weight.shape
    questions = rows // QLEN
    slot_rows = rows // NEED
    half = depth // 2
    chunks = chunk_list(rows)
    count = len(chunks)
    dma = pltpu.SemaphoreType.DMA
    vmem, anywhere = pl.BlockSpec(memory_space=pltpu.VMEM), pl.BlockSpec(memory_space=pl.ANY)
    ordered, place = pl.pallas_call(
        functools.partial(exchange, lax.axis_size("serve"), chunks),
        out_shape=(
            jax.ShapeDtypeStruct((rows, out_cols), BF16),
            jax.ShapeDtypeStruct((1, questions), jnp.int32),
        ),
        in_specs=[anywhere, anywhere, vmem, vmem, anywhere],
        out_specs=(anywhere, vmem),
        scratch_shapes=[
            pltpu.VMEM((rows, cols), BF16),
            pltpu.VMEM((rows, cols), BF16),
            pltpu.VMEM((rows - slot_rows, cols), BF16),
            pltpu.VMEM((rows - slot_rows, cols), BF16),
            pltpu.VMEM((SHARE * piece, width), BF16),
            pltpu.VMEM((RING, rows, cols), BF16),
            pltpu.VMEM((half, out_cols), BF16),
            pltpu.VMEM((half, out_cols), BF16),
            pltpu.VMEM((rows, out_cols), F32),
            pltpu.VMEM((rows, out_cols), BF16),
            pltpu.VMEM((rows, out_cols), BF16),
            pltpu.VMEM((rows, out_cols), BF16),
            pltpu.VMEM((rows, 1), F32),
            dma((3,)), dma((count,)),
            dma((3,)), dma((3,)), dma((3,)), dma((3,)),
            dma((count,)), dma((count,)), dma((count,)), dma((count,)),
            dma((2,)), dma((2,)), dma((2,)), dma((2,)),
            dma((count, 4)), dma((count, 4)), dma((count, 4)), dma((count, 4)),
            dma((count,)), dma((count,)),
        ],
        compiler_params=pltpu.CompilerParams(
            collective_id=0, has_side_effects=True, vmem_limit_bytes=VMEM_LIMIT),
        name="exchange",
    )(queries, kv_cache.reshape(piece, width), question_slot.reshape(1, questions),
      question_len.reshape(1, questions), out_weight)
    return pl.pallas_call(
        unsort,
        out_shape=jax.ShapeDtypeStruct((rows, out_cols), BF16),
        in_specs=[pl.BlockSpec(memory_space=pltpu.SMEM), anywhere],
        out_specs=anywhere,
        scratch_shapes=[pltpu.VMEM((rows, out_cols), BF16), dma((questions,)), dma((questions,))],
        name="unsort",
    )(place.reshape(questions), ordered)


def solution(mesh):
    return jax.shard_map(
        on_device,
        mesh=mesh,
        in_specs=(
            P("serve", "tensor"),
            P("serve", "tensor", None),
            P("serve"),
            P("serve"),
            P(None, "tensor"),
        ),
        out_specs=P("serve", "tensor"),
        check_vma=False,
    )
```

```python
import functools

import jax
import jax.numpy as jnp
from jax import lax
from jax.experimental import pallas as pl
from jax.experimental.pallas import tpu as pltpu
from jax.sharding import PartitionSpec as P

QLEN = 32
NEED = 4
RING = 8
SHARE = 4
LANES = 8
HEAD_DIM = 128
MESH = pl.DeviceIdType.MESH
F32 = jnp.float32
BF16 = jnp.bfloat16
VMEM_LIMIT = 56 * 1024 * 1024


def remote(src, dst, send, recv, device):
    return pltpu.make_async_remote_copy(
        src_ref=src, dst_ref=dst, send_sem=send, recv_sem=recv,
        device_id=device, device_id_type=MESH)


def greet(partners):
    barrier = pltpu.get_barrier_semaphore()
    for device in partners:
        pl.semaphore_signal(barrier, inc=1, device_id=device, device_id_type=MESH)
    return lambda: pl.semaphore_wait(barrier, len(partners))


def attend(q_ref, kvb, o_ref):
    for h in range(q_ref.shape[1] // HEAD_DIM):
        query = q_ref[:, h * HEAD_DIM:(h + 1) * HEAD_DIM]
        scores = lax.dot_general(query, kvb[:, :HEAD_DIM], (((1,), (1,)), ((), ())),
                                 preferred_element_type=F32)
        top = jnp.max(scores, axis=1, keepdims=True)
        exps = jnp.exp((scores - top) * HEAD_DIM ** -0.5)
        total = jnp.sum(exps, axis=1, keepdims=True)
        blend = jnp.dot(exps.astype(BF16), kvb[:, HEAD_DIM:], preferred_element_type=F32)
        o_ref[:, h * HEAD_DIM:(h + 1) * HEAD_DIM] = (blend / total).astype(BF16)


def chunk_list(rows):
    sub = rows // (2 * NEED)
    chunks = [(i * sub, sub, i // 2) for i in range(2 * NEED - 1)]
    return chunks + [(rows - sub, sub // 2, NEED - 1), (rows - sub // 2, sub // 2, NEED - 1)]


def exchange(n_serve, chunks, q_hbm, kv_hbm, slot_ref, len_ref, w_hbm, out_hbm, place_out,
             qv, sq, vq, ao, kvb, g, wo, wp, acc, ps, pr, ob, live_ref,
             local_sem, ob_sem, kv_sr, kv_rr, kv_sl, kv_rl, q_s, q_r, ret_s, ret_r,
             w_s, w_r, ag_sr, ag_rr, ag_sl, ag_rl, p_s, p_r):
    s = lax.axis_index("serve")
    t = lax.axis_index("tensor")
    y = lax.rem(t, RING)
    z = t // RING
    p = lax.rem(t, SHARE)
    core = lax.rem(s, 2)
    right = (s, z * RING + lax.rem(y + 1, RING))
    left = (s, z * RING + lax.rem(y + RING - 1, RING))
    mate = (s, lax.rem(t + RING, 2 * RING))
    sibling = (s + 1 - 2 * core, t)
    owner = [None] + [(lax.rem(s + n_serve - j, n_serve), t) for j in range(1, NEED)]
    asker = [None] + [(lax.rem(s + j, n_serve), t) for j in range(1, NEED)]
    rows, cols = q_hbm.shape
    questions = rows // QLEN
    slot_rows = rows // NEED
    piece = kv_hbm.shape[0]
    half, out_cols = wo.shape
    wpart = half // LANES

    lane = lax.rem(s, LANES)
    x = lane // 2
    x_up = (s - lane + lax.rem(lane + 2, LANES), t)
    x_down = (s - lane + lax.rem(lane + LANES - 2, LANES), t)

    wait_entry = greet([owner[3], asker[3], owner[2], asker[2], owner[1], asker[1],
                        x_up, x_down, mate, right, left])
    q_load = pltpu.make_async_copy(q_hbm, qv, local_sem.at[0])
    q_load.start()

    def kv_rows(index):
        return kvb.at[pl.ds(pl.multiple_of(index * piece, 16), piece), :]

    kv_load = pltpu.make_async_copy(kv_hbm, kv_rows(p), local_sem.at[1])
    kv_load.start()
    w_load = pltpu.make_async_copy(
        w_hbm.at[pl.ds(pl.multiple_of(z * half, half), half), :], wo, local_sem.at[2])
    w_load.start()
    wait_entry()

    def kv_right(k):
        src = kv_hbm if k == 0 else kv_rows(p - k)
        return remote(src, kv_rows(p - k), kv_sr.at[k], kv_rr.at[k], right)

    def kv_left(k):
        src = kv_hbm if k == 0 else kv_rows(p + k)
        return remote(src, kv_rows(p + k), kv_sl.at[k], kv_rl.at[k], left)

    @pl.when(p < SHARE - 1)
    def _():
        kv_right(0).start()

    @pl.when(p > 0)
    def _():
        kv_left(0).start()

    def kv_step(k):
        @pl.when(p >= k)
        def _():
            dst = kv_rows(p - k)
            remote(dst, dst, kv_sr.at[k - 1], kv_rr.at[k - 1], left).wait_recv()
            if k < SHARE - 1:
                @pl.when(p < SHARE - 1)
                def _():
                    kv_right(k).start()

        @pl.when(p + k < SHARE)
        def _():
            dst = kv_rows(p + k)
            remote(dst, dst, kv_sl.at[k - 1], kv_rl.at[k - 1], right).wait_recv()
            if k < SHARE - 1:
                @pl.when(p > 0)
                def _():
                    kv_left(k).start()

    slot = slot_ref[...]
    mine = (lax.broadcasted_iota(jnp.int32, (8, questions), 0) == slot).astype(F32)
    before = (lax.broadcasted_iota(jnp.int32, (questions, questions), 0)
              < lax.broadcasted_iota(jnp.int32, (questions, questions), 1)).astype(F32)
    rank = jnp.dot(mine.astype(BF16), before.astype(BF16), preferred_element_type=F32)
    place = jnp.sum(mine * rank, axis=0, keepdims=True) + slot.astype(F32) * (questions // NEED)
    spread = (lax.broadcasted_iota(jnp.int32, (questions, rows), 1) // QLEN
              == lax.broadcasted_iota(jnp.int32, (questions, rows), 0)).astype(BF16)
    both = jnp.concatenate([place, len_ref[...].astype(F32), jnp.zeros((6, questions), F32)], axis=0)
    both = jnp.dot(both.astype(BF16), spread, preferred_element_type=F32).astype(jnp.int32)
    token = lax.broadcasted_iota(jnp.int32, (1, rows), 1) % QLEN
    row = both[0:1, :] * QLEN + token
    live = (token < both[1:2, :]).astype(F32)
    place_out[...] = place.astype(jnp.int32)

    q_load.wait()

    def sort(j):
        first = j * slot_rows
        chosen = (lax.broadcasted_iota(jnp.int32, (slot_rows, rows), 0) + first == row).astype(F32)
        sq[pl.ds(first, slot_rows), :] = jnp.dot(
            chosen.astype(BF16), qv[...], preferred_element_type=F32).astype(BF16)
        live_ref[pl.ds(first, slot_rows), :] = jnp.sum(chosen * live, axis=1, keepdims=True)

    def spot(c):
        first, size, _ = chunks[c]
        return pl.ds(first - slot_rows, size)

    def part_of(ref, c):
        first, size, _ = chunks[c]
        return ref.at[pl.ds(first, size), :]

    def ask(c):
        return remote(part_of(sq, c), vq.at[spot(c), :], q_s.at[c], q_r.at[c], owner[chunks[c][2]])

    def w_part(x_from, side, low=0, size=None):
        first = (lax.rem(x_from + LANES, LANES // 2) * 2 + side) * wpart + low
        return wp.at[pl.ds(pl.multiple_of(first, wpart // 2), size or wpart), :]

    def w_send(i, x_from, side, device, low=0, size=None):
        part = w_part(x_from, side, low, size)
        return remote(part, part, w_s.at[i], w_r.at[i], device)

    w_first = (1 - z) * half + lane * wpart
    w_out = remote(w_hbm.at[pl.ds(pl.multiple_of(w_first, wpart), wpart), :], w_part(x, core),
                   w_s.at[0], w_r.at[0], mate)
    lower = wpart // 2
    w_sends = [
        w_out,
        w_send(1, x, core, x_up), w_send(2, x, core, x_down), w_send(3, x, core, sibling),
        w_send(4, x - 1, core, x_up, 0, lower), w_send(5, x - 1, core, sibling),
        w_send(6, x + 1, core, x_down, lower, lower), w_send(7, x + 1, core, sibling),
        w_send(8, x + 2, core, sibling, 0, lower), w_send(9, x + 2, core, sibling, lower, lower),
    ]

    def w_stage(i):
        if i == 0:
            w_out.wait_recv()
            for n in (1, 2, 3):
                w_sends[n].start()
        elif i == 1:
            w_send(1, x - 1, core, x_down).wait_recv()
            w_sends[4].start()
            w_sends[5].start()
            w_send(2, x + 1, core, x_up).wait_recv()
            w_sends[6].start()
            w_sends[7].start()
        else:
            w_send(4, x + 2, core, x_down, 0, lower).wait_recv()
            w_sends[8].start()
            w_send(6, x + 2, core, x_up, lower, lower).wait_recv()
            w_sends[9].start()

    def w_ready():
        w_load.wait()
        w_send(3, x, 1 - core, sibling).wait_recv()
        w_send(5, x - 1, 1 - core, sibling).wait_recv()
        w_send(7, x + 1, 1 - core, sibling).wait_recv()
        w_send(8, x + 2, 1 - core, sibling, 0, lower).wait_recv()
        w_send(9, x + 2, 1 - core, sibling, lower, lower).wait_recv()

    count = len(chunks)
    visitors = [c for c in range(count) if chunks[c][2] > 0]
    for j in range(1, NEED):
        sort(j)
        for c in visitors:
            if chunks[c][2] == j:
                ask(c).start()
    w_out.start()
    kv_step(1)
    sort(0)
    kv_step(2)
    w_stage(0)
    kv_step(3)
    kv_load.wait()

    reach_right = [4 if c % 2 == 0 else 3 for c in range(len(chunks))]
    reach_left = [3 if c % 2 == 0 else 4 for c in range(len(chunks))]

    def block(origin, c):
        first, size, _ = chunks[c]
        return g.at[lax.rem(origin + RING, RING), pl.ds(first, size), :]

    def go_right(c, k):
        return remote(block(y - k, c), block(y - k, c),
                      ag_sr.at[c, k], ag_rr.at[c, k], right)

    def go_left(c, k):
        return remote(block(y + k, c), block(y + k, c),
                      ag_sl.at[c, k], ag_rl.at[c, k], left)

    def from_left(c, k):
        part = block(y - k, c)
        return remote(part, part, ag_sr.at[c, k - 1], ag_rr.at[c, k - 1], left)

    def from_right(c, k):
        part = block(y + k, c)
        return remote(part, part, ag_sl.at[c, k - 1], ag_rl.at[c, k - 1], right)

    def answer(c):
        return remote(ao.at[spot(c), :], block(y, c), ret_s.at[c], ret_r.at[c], asker[chunks[c][2]])

    def visit(c):
        slot = chunks[c][2]
        remote(vq.at[spot(c), :], vq.at[spot(c), :], q_s.at[c], q_r.at[c], asker[slot]).wait_recv()
        attend(vq.at[spot(c), :], kvb, ao.at[spot(c), :])
        answer(c).start()

    def partial(c):
        return remote(part_of(ps, c), part_of(pr, c), p_s.at[c], p_r.at[c], mate)

    def project(c):
        first, size, slot = chunks[c]
        lhs = jnp.concatenate([g[i, first:first + size, :] for i in range(RING)], axis=1)
        ps[first:first + size, :] = jnp.dot(lhs, wp[...], preferred_element_type=F32).astype(BF16)
        partial(c).start()
        acc[first:first + size, :] = jnp.dot(lhs, wo[...], preferred_element_type=F32)

    def write(c):
        return pltpu.make_async_copy(part_of(ob, c), part_of(out_hbm, c), ob_sem.at[c])

    def finish(c):
        first, size, _ = chunks[c]
        partial(c).wait_recv()
        part = slice(first, first + size)
        total = acc[part, :] + pr[part, :].astype(F32)
        ob[part, :] = jnp.where(live_ref[part, :] > 0.5, total, 0.0).astype(BF16)
        write(c).start()

    def start(c):
        if chunks[c][2] > 0:
            part = block(y, c)
            remote(part, part, ret_s.at[c], ret_r.at[c], owner[chunks[c][2]]).wait_recv()
        else:
            attend(part_of(sq, c), kvb, block(y, c))
        go_right(c, 0).start()
        go_left(c, 0).start()

    def step(c, k):
        if k <= reach_right[c]:
            from_left(c, k).wait_recv()
            if k < reach_right[c]:
                go_right(c, k).start()
        if k <= reach_left[c]:
            from_right(c, k).wait_recv()
            if k < reach_left[c]:
                go_left(c, k).start()

    tasks = []
    ready = {}
    for c, (first, size, slot) in enumerate(chunks):
        begin = 3.5 * first
        if slot > 0:
            tasks.append((begin, functools.partial(start, c)))
        for k in range(1, 5):
            tasks.append((begin + LAG * k * max(size, 96), functools.partial(step, c, k)))
        ready[c] = max(begin + LAG * 4 * max(size, 96) + 1, W_TIME + 2 + c)
        tasks.append((ready[c], functools.partial(project, c)))
        tasks.append((ready[c] + 450 if c < count - 1 else 1e9, functools.partial(finish, c)))
    for i, c in enumerate(visitors):
        tasks.append((VISIT[chunks[c][2]] + i, functools.partial(visit, c)))
    for i in (1, 2):
        tasks.append((W_STAGE[i - 1], functools.partial(w_stage, i)))
    tasks.append((W_TIME + 1, w_ready))
    tasks.sort(key=lambda task: task[0])
    start(0)
    start(1)
    for _, task in tasks:
        task()

    for k in range(SHARE - 1):
        @pl.when(jnp.logical_and(p >= k, p < SHARE - 1))
        def _(k=k):
            kv_right(k).wait_send()

        @pl.when(jnp.logical_and(p + k < SHARE, p > 0))
        def _(k=k):
            kv_left(k).wait_send()
    for c in visitors:
        ask(c).wait_send()
        answer(c).wait_send()
    for copy in w_sends:
        copy.wait_send()
    for c in range(count):
        for k in range(reach_right[c]):
            go_right(c, k).wait_send()
        for k in range(reach_left[c]):
            go_left(c, k).wait_send()
        partial(c).wait_send()
        write(c).wait()


LAG = 3.0
W_TIME = 2000
W_STAGE = [900, 1500]
VISIT = [0, 10, 310, 620]


def unsort(place_ref, ordered, out, held, in_sem, out_sem):
    questions = place_ref.shape[0]

    def fetch(q):
        return pltpu.make_async_copy(
            ordered.at[pl.ds(pl.multiple_of(place_ref[q] * QLEN, QLEN), QLEN), :],
            held.at[pl.ds(q * QLEN, QLEN), :], in_sem.at[q])

    def store(q):
        part = pl.ds(q * QLEN, QLEN)
        return pltpu.make_async_copy(held.at[part, :], out.at[part, :], out_sem.at[q])

    for q in range(questions):
        fetch(q).start()
    for q in range(questions):
        fetch(q).wait()
        store(q).start()
    for q in range(questions):
        store(q).wait()


def on_device(queries, kv_cache, question_slot, question_len, out_weight):
    rows, cols = queries.shape
    piece, width = kv_cache.shape[1:]
    depth, out_cols = out_weight.shape
    questions = rows // QLEN
    slot_rows = rows // NEED
    half = depth // 2
    chunks = chunk_list(rows)
    count = len(chunks)
    dma = pltpu.SemaphoreType.DMA
    vmem, anywhere = pl.BlockSpec(memory_space=pltpu.VMEM), pl.BlockSpec(memory_space=pl.ANY)
    ordered, place = pl.pallas_call(
        functools.partial(exchange, lax.axis_size("serve"), chunks),
        out_shape=(
            jax.ShapeDtypeStruct((rows, out_cols), BF16),
            jax.ShapeDtypeStruct((1, questions), jnp.int32),
        ),
        in_specs=[anywhere, anywhere, vmem, vmem, anywhere],
        out_specs=(anywhere, vmem),
        scratch_shapes=[
            pltpu.VMEM((rows, cols), BF16),
            pltpu.VMEM((rows, cols), BF16),
            pltpu.VMEM((rows - slot_rows, cols), BF16),
            pltpu.VMEM((rows - slot_rows, cols), BF16),
            pltpu.VMEM((SHARE * piece, width), BF16),
            pltpu.VMEM((RING, rows, cols), BF16),
            pltpu.VMEM((half, out_cols), BF16),
            pltpu.VMEM((half, out_cols), BF16),
            pltpu.VMEM((rows, out_cols), F32),
            pltpu.VMEM((rows, out_cols), BF16),
            pltpu.VMEM((rows, out_cols), BF16),
            pltpu.VMEM((rows, out_cols), BF16),
            pltpu.VMEM((rows, 1), F32),
            dma((3,)), dma((count,)),
            dma((3,)), dma((3,)), dma((3,)), dma((3,)),
            dma((count,)), dma((count,)), dma((count,)), dma((count,)),
            dma((10,)), dma((10,)),
            dma((count, 4)), dma((count, 4)), dma((count, 4)), dma((count, 4)),
            dma((count,)), dma((count,)),
        ],
        compiler_params=pltpu.CompilerParams(
            collective_id=0, has_side_effects=True, vmem_limit_bytes=VMEM_LIMIT),
        name="exchange",
    )(queries, kv_cache.reshape(piece, width), question_slot.reshape(1, questions),
      question_len.reshape(1, questions), out_weight)
    return pl.pallas_call(
        unsort,
        out_shape=jax.ShapeDtypeStruct((rows, out_cols), BF16),
        in_specs=[pl.BlockSpec(memory_space=pltpu.SMEM), anywhere],
        out_specs=anywhere,
        scratch_shapes=[pltpu.VMEM((rows, out_cols), BF16), dma((questions,)), dma((questions,))],
        name="unsort",
    )(place.reshape(questions), ordered)


def solution(mesh):
    return jax.shard_map(
        on_device,
        mesh=mesh,
        in_specs=(
            P("serve", "tensor"),
            P("serve", "tensor", None),
            P("serve"),
            P("serve"),
            P(None, "tensor"),
        ),
        out_specs=P("serve", "tensor"),
        check_vma=False,
    )
```

```python
import functools

import jax
import jax.numpy as jnp
from jax import lax
from jax.experimental import pallas as pl
from jax.experimental.pallas import tpu as pltpu
from jax.sharding import PartitionSpec as P

QLEN = 32
NEED = 4
RING = 8
SHARE = 4
LANES = 8
HEAD_DIM = 128
MESH = pl.DeviceIdType.MESH
F32 = jnp.float32
BF16 = jnp.bfloat16
VMEM_LIMIT = 56 * 1024 * 1024


def remote(src, dst, send, recv, device):
    return pltpu.make_async_remote_copy(
        src_ref=src, dst_ref=dst, send_sem=send, recv_sem=recv,
        device_id=device, device_id_type=MESH)


def greet(partners):
    barrier = pltpu.get_barrier_semaphore()
    for device in partners:
        pl.semaphore_signal(barrier, inc=1, device_id=device, device_id_type=MESH)
    return lambda: pl.semaphore_wait(barrier, len(partners))


def attend(q_ref, kvb, o_ref):
    for h in range(q_ref.shape[1] // HEAD_DIM):
        query = q_ref[:, h * HEAD_DIM:(h + 1) * HEAD_DIM]
        scores = lax.dot_general(query, kvb[:, :HEAD_DIM], (((1,), (1,)), ((), ())),
                                 preferred_element_type=F32)
        top = jnp.max(scores, axis=1, keepdims=True)
        exps = jnp.exp((scores - top) * HEAD_DIM ** -0.5)
        total = jnp.sum(exps, axis=1, keepdims=True)
        blend = jnp.dot(exps.astype(BF16), kvb[:, HEAD_DIM:], preferred_element_type=F32)
        o_ref[:, h * HEAD_DIM:(h + 1) * HEAD_DIM] = (blend / total).astype(BF16)


def chunk_list(rows):
    sub = rows // (2 * NEED)
    chunks = [(i * sub, sub, i // 2) for i in range(2 * NEED - 1)]
    return chunks + [(rows - sub, sub // 2, NEED - 1), (rows - sub // 2, sub // 2, NEED - 1)]


def exchange(n_serve, chunks, q_hbm, kv_hbm, slot_ref, len_ref, w_hbm, out_hbm, place_out,
             qv, sq, vq, ao, kvb, g, wo, wp, acc, ps, pr, ob, live_ref,
             local_sem, ob_sem, kv_sr, kv_rr, kv_sl, kv_rl, q_s, q_r, ret_s, ret_r,
             w_s, w_r, ag_sr, ag_rr, ag_sl, ag_rl, p_s, p_r):
    s = lax.axis_index("serve")
    t = lax.axis_index("tensor")
    y = lax.rem(t, RING)
    z = t // RING
    p = lax.rem(t, SHARE)
    core = lax.rem(s, 2)
    right = (s, z * RING + lax.rem(y + 1, RING))
    left = (s, z * RING + lax.rem(y + RING - 1, RING))
    mate = (s, lax.rem(t + RING, 2 * RING))
    sibling = (s + 1 - 2 * core, t)
    owner = [None] + [(lax.rem(s + n_serve - j, n_serve), t) for j in range(1, NEED)]
    asker = [None] + [(lax.rem(s + j, n_serve), t) for j in range(1, NEED)]
    rows, cols = q_hbm.shape
    questions = rows // QLEN
    slot_rows = rows // NEED
    piece = kv_hbm.shape[0]
    half, out_cols = wo.shape
    wpart = half // LANES

    lane = lax.rem(s, LANES)
    x = lane // 2
    x_up = (s - lane + lax.rem(lane + 2, LANES), t)
    x_down = (s - lane + lax.rem(lane + LANES - 2, LANES), t)

    wait_entry = greet([owner[3], asker[3], owner[2], asker[2], owner[1], asker[1],
                        x_up, x_down, mate, right, left])
    q_load = pltpu.make_async_copy(q_hbm, qv, local_sem.at[0])
    q_load.start()

    def kv_rows(index):
        return kvb.at[pl.ds(pl.multiple_of(index * piece, 16), piece), :]

    kv_load = pltpu.make_async_copy(kv_hbm, kv_rows(p), local_sem.at[1])
    kv_load.start()
    w_load = pltpu.make_async_copy(
        w_hbm.at[pl.ds(pl.multiple_of(z * half, half), half), :], wo, local_sem.at[2])
    w_load.start()
    wait_entry()

    def kv_right(k):
        src = kv_hbm if k == 0 else kv_rows(p - k)
        return remote(src, kv_rows(p - k), kv_sr.at[k], kv_rr.at[k], right)

    def kv_left(k):
        src = kv_hbm if k == 0 else kv_rows(p + k)
        return remote(src, kv_rows(p + k), kv_sl.at[k], kv_rl.at[k], left)

    @pl.when(p < SHARE - 1)
    def _():
        kv_right(0).start()

    @pl.when(p > 0)
    def _():
        kv_left(0).start()

    def kv_step(k):
        @pl.when(p >= k)
        def _():
            dst = kv_rows(p - k)
            remote(dst, dst, kv_sr.at[k - 1], kv_rr.at[k - 1], left).wait_recv()
            if k < SHARE - 1:
                @pl.when(p < SHARE - 1)
                def _():
                    kv_right(k).start()

        @pl.when(p + k < SHARE)
        def _():
            dst = kv_rows(p + k)
            remote(dst, dst, kv_sl.at[k - 1], kv_rl.at[k - 1], right).wait_recv()
            if k < SHARE - 1:
                @pl.when(p > 0)
                def _():
                    kv_left(k).start()

    slot = slot_ref[...]
    mine = (lax.broadcasted_iota(jnp.int32, (8, questions), 0) == slot).astype(F32)
    before = (lax.broadcasted_iota(jnp.int32, (questions, questions), 0)
              < lax.broadcasted_iota(jnp.int32, (questions, questions), 1)).astype(F32)
    rank = jnp.dot(mine.astype(BF16), before.astype(BF16), preferred_element_type=F32)
    place = jnp.sum(mine * rank, axis=0, keepdims=True) + slot.astype(F32) * (questions // NEED)
    spread = (lax.broadcasted_iota(jnp.int32, (questions, rows), 1) // QLEN
              == lax.broadcasted_iota(jnp.int32, (questions, rows), 0)).astype(BF16)
    both = jnp.concatenate([place, len_ref[...].astype(F32), jnp.zeros((6, questions), F32)], axis=0)
    both = jnp.dot(both.astype(BF16), spread, preferred_element_type=F32).astype(jnp.int32)
    token = lax.broadcasted_iota(jnp.int32, (1, rows), 1) % QLEN
    row = both[0:1, :] * QLEN + token
    live = (token < both[1:2, :]).astype(F32)
    place_out[...] = place.astype(jnp.int32)

    q_load.wait()

    def sort(j):
        first = j * slot_rows
        chosen = (lax.broadcasted_iota(jnp.int32, (slot_rows, rows), 0) + first == row).astype(F32)
        sq[pl.ds(first, slot_rows), :] = jnp.dot(
            chosen.astype(BF16), qv[...], preferred_element_type=F32).astype(BF16)
        live_ref[pl.ds(first, slot_rows), :] = jnp.sum(chosen * live, axis=1, keepdims=True)

    def spot(c):
        first, size, _ = chunks[c]
        return pl.ds(first - slot_rows, size)

    def part_of(ref, c):
        first, size, _ = chunks[c]
        return ref.at[pl.ds(first, size), :]

    def ask(c):
        return remote(part_of(sq, c), vq.at[spot(c), :], q_s.at[c], q_r.at[c], owner[chunks[c][2]])

    def w_part(x_from, side, low=0, size=None):
        first = (lax.rem(x_from + LANES, LANES // 2) * 2 + side) * wpart + low
        return wp.at[pl.ds(pl.multiple_of(first, wpart // 2), size or wpart), :]

    def w_send(i, x_from, side, device, low=0, size=None):
        part = w_part(x_from, side, low, size)
        return remote(part, part, w_s.at[i], w_r.at[i], device)

    w_first = (1 - z) * half + lane * wpart
    w_out = remote(w_hbm.at[pl.ds(pl.multiple_of(w_first, wpart), wpart), :], w_part(x, core),
                   w_s.at[0], w_r.at[0], mate)
    lower = wpart // 2
    w_sends = [
        w_out,
        w_send(1, x, core, x_up), w_send(2, x, core, x_down), w_send(3, x, core, sibling),
        w_send(4, x - 1, core, x_up, 0, lower), w_send(5, x - 1, core, sibling),
        w_send(6, x + 1, core, x_down, lower, lower), w_send(7, x + 1, core, sibling),
        w_send(8, x + 2, core, sibling, 0, lower), w_send(9, x + 2, core, sibling, lower, lower),
    ]

    def w_stage(i):
        if i == 0:
            w_out.wait_recv()
            for n in (1, 2, 3):
                w_sends[n].start()
        elif i == 1:
            w_send(1, x - 1, core, x_down).wait_recv()
            w_sends[4].start()
            w_sends[5].start()
            w_send(2, x + 1, core, x_up).wait_recv()
            w_sends[6].start()
            w_sends[7].start()
        else:
            w_send(4, x + 2, core, x_down, 0, lower).wait_recv()
            w_sends[8].start()
            w_send(6, x + 2, core, x_up, lower, lower).wait_recv()
            w_sends[9].start()

    def w_ready():
        w_load.wait()
        w_send(3, x, 1 - core, sibling).wait_recv()
        w_send(5, x - 1, 1 - core, sibling).wait_recv()
        w_send(7, x + 1, 1 - core, sibling).wait_recv()
        w_send(8, x + 2, 1 - core, sibling, 0, lower).wait_recv()
        w_send(9, x + 2, 1 - core, sibling, lower, lower).wait_recv()

    count = len(chunks)
    visitors = [c for c in range(count) if chunks[c][2] > 0]
    for j in range(1, NEED):
        sort(j)
        for c in visitors:
            if chunks[c][2] == j:
                ask(c).start()
    w_out.start()
    kv_step(1)
    sort(0)
    kv_step(2)
    w_stage(0)
    kv_step(3)
    kv_load.wait()

    reach_right = [4 if c % 2 == 0 else 3 for c in range(len(chunks))]
    reach_left = [3 if c % 2 == 0 else 4 for c in range(len(chunks))]

    def block(origin, c):
        first, size, _ = chunks[c]
        return g.at[lax.rem(origin + RING, RING), pl.ds(first, size), :]

    def go_right(c, k):
        return remote(block(y - k, c), block(y - k, c),
                      ag_sr.at[c, k], ag_rr.at[c, k], right)

    def go_left(c, k):
        return remote(block(y + k, c), block(y + k, c),
                      ag_sl.at[c, k], ag_rl.at[c, k], left)

    def from_left(c, k):
        part = block(y - k, c)
        return remote(part, part, ag_sr.at[c, k - 1], ag_rr.at[c, k - 1], left)

    def from_right(c, k):
        part = block(y + k, c)
        return remote(part, part, ag_sl.at[c, k - 1], ag_rl.at[c, k - 1], right)

    def answer(c):
        return remote(ao.at[spot(c), :], block(y, c), ret_s.at[c], ret_r.at[c], asker[chunks[c][2]])

    def visit(c):
        slot = chunks[c][2]
        remote(vq.at[spot(c), :], vq.at[spot(c), :], q_s.at[c], q_r.at[c], asker[slot]).wait_recv()
        attend(vq.at[spot(c), :], kvb, ao.at[spot(c), :])
        answer(c).start()

    def partial(c):
        return remote(part_of(ps, c), part_of(pr, c), p_s.at[c], p_r.at[c], mate)

    def project(c):
        first, size, slot = chunks[c]
        lhs = jnp.concatenate([g[i, first:first + size, :] for i in range(RING)], axis=1)
        ps[first:first + size, :] = jnp.dot(lhs, wp[...], preferred_element_type=F32).astype(BF16)
        partial(c).start()
        acc[first:first + size, :] = jnp.dot(lhs, wo[...], preferred_element_type=F32)

    def write(c):
        return pltpu.make_async_copy(part_of(ob, c), part_of(out_hbm, c), ob_sem.at[c])

    def finish(c):
        first, size, _ = chunks[c]
        partial(c).wait_recv()
        part = slice(first, first + size)
        total = acc[part, :] + pr[part, :].astype(F32)
        ob[part, :] = jnp.where(live_ref[part, :] > 0.5, total, 0.0).astype(BF16)
        write(c).start()

    def start(c):
        if chunks[c][2] > 0:
            part = block(y, c)
            remote(part, part, ret_s.at[c], ret_r.at[c], owner[chunks[c][2]]).wait_recv()
        else:
            attend(part_of(sq, c), kvb, block(y, c))
        go_right(c, 0).start()
        go_left(c, 0).start()

    def step(c, k):
        if k <= reach_right[c]:
            from_left(c, k).wait_recv()
            if k < reach_right[c]:
                go_right(c, k).start()
        if k <= reach_left[c]:
            from_right(c, k).wait_recv()
            if k < reach_left[c]:
                go_left(c, k).start()

    tasks = []
    ready = {}
    for c, (first, size, slot) in enumerate(chunks):
        begin = 3.5 * first
        if slot > 0:
            tasks.append((begin, functools.partial(start, c)))
        for k in range(1, 5):
            tasks.append((begin + LAG * k * max(size, 96), functools.partial(step, c, k)))
        ready[c] = max(begin + LAG * 4 * max(size, 96) + 1, W_TIME + 2 + c)
        tasks.append((ready[c], functools.partial(project, c)))
        tasks.append((ready[c] + 450 if c < count - 1 else 1e9, functools.partial(finish, c)))
    for i, c in enumerate(visitors):
        tasks.append((VISIT[chunks[c][2]] + i, functools.partial(visit, c)))
    for i in (1, 2):
        tasks.append((W_STAGE[i - 1], functools.partial(w_stage, i)))
    tasks.append((W_TIME + 1, w_ready))
    tasks.sort(key=lambda task: task[0])
    start(0)
    start(1)
    for _, task in tasks:
        task()

    for k in range(SHARE - 1):
        @pl.when(jnp.logical_and(p >= k, p < SHARE - 1))
        def _(k=k):
            kv_right(k).wait_send()

        @pl.when(jnp.logical_and(p + k < SHARE, p > 0))
        def _(k=k):
            kv_left(k).wait_send()
    for c in visitors:
        ask(c).wait_send()
        answer(c).wait_send()
    for copy in w_sends:
        copy.wait_send()
    for c in range(count):
        for k in range(reach_right[c]):
            go_right(c, k).wait_send()
        for k in range(reach_left[c]):
            go_left(c, k).wait_send()
        partial(c).wait_send()
        write(c).wait()


LAG = 3.0
W_TIME = 2000
W_STAGE = [900, 1500]
VISIT = [0, 10, 650, 1300]


def unsort(place_ref, ordered, out, held, in_sem, out_sem):
    questions = place_ref.shape[0]

    def fetch(q):
        return pltpu.make_async_copy(
            ordered.at[pl.ds(pl.multiple_of(place_ref[q] * QLEN, QLEN), QLEN), :],
            held.at[pl.ds(q * QLEN, QLEN), :], in_sem.at[q])

    def store(q):
        part = pl.ds(q * QLEN, QLEN)
        return pltpu.make_async_copy(held.at[part, :], out.at[part, :], out_sem.at[q])

    for q in range(questions):
        fetch(q).start()
    for q in range(questions):
        fetch(q).wait()
        store(q).start()
    for q in range(questions):
        store(q).wait()


def on_device(queries, kv_cache, question_slot, question_len, out_weight):
    rows, cols = queries.shape
    piece, width = kv_cache.shape[1:]
    depth, out_cols = out_weight.shape
    questions = rows // QLEN
    slot_rows = rows // NEED
    half = depth // 2
    chunks = chunk_list(rows)
    count = len(chunks)
    dma = pltpu.SemaphoreType.DMA
    vmem, anywhere = pl.BlockSpec(memory_space=pltpu.VMEM), pl.BlockSpec(memory_space=pl.ANY)
    ordered, place = pl.pallas_call(
        functools.partial(exchange, lax.axis_size("serve"), chunks),
        out_shape=(
            jax.ShapeDtypeStruct((rows, out_cols), BF16),
            jax.ShapeDtypeStruct((1, questions), jnp.int32),
        ),
        in_specs=[anywhere, anywhere, vmem, vmem, anywhere],
        out_specs=(anywhere, vmem),
        scratch_shapes=[
            pltpu.VMEM((rows, cols), BF16),
            pltpu.VMEM((rows, cols), BF16),
            pltpu.VMEM((rows - slot_rows, cols), BF16),
            pltpu.VMEM((rows - slot_rows, cols), BF16),
            pltpu.VMEM((SHARE * piece, width), BF16),
            pltpu.VMEM((RING, rows, cols), BF16),
            pltpu.VMEM((half, out_cols), BF16),
            pltpu.VMEM((half, out_cols), BF16),
            pltpu.VMEM((rows, out_cols), F32),
            pltpu.VMEM((rows, out_cols), BF16),
            pltpu.VMEM((rows, out_cols), BF16),
            pltpu.VMEM((rows, out_cols), BF16),
            pltpu.VMEM((rows, 1), F32),
            dma((3,)), dma((count,)),
            dma((3,)), dma((3,)), dma((3,)), dma((3,)),
            dma((count,)), dma((count,)), dma((count,)), dma((count,)),
            dma((10,)), dma((10,)),
            dma((count, 4)), dma((count, 4)), dma((count, 4)), dma((count, 4)),
            dma((count,)), dma((count,)),
        ],
        compiler_params=pltpu.CompilerParams(
            collective_id=0, has_side_effects=True, vmem_limit_bytes=VMEM_LIMIT),
        name="exchange",
    )(queries, kv_cache.reshape(piece, width), question_slot.reshape(1, questions),
      question_len.reshape(1, questions), out_weight)
    return pl.pallas_call(
        unsort,
        out_shape=jax.ShapeDtypeStruct((rows, out_cols), BF16),
        in_specs=[pl.BlockSpec(memory_space=pltpu.SMEM), anywhere],
        out_specs=anywhere,
        scratch_shapes=[pltpu.VMEM((rows, out_cols), BF16), dma((questions,)), dma((questions,))],
        name="unsort",
    )(place.reshape(questions), ordered)


def solution(mesh):
    return jax.shard_map(
        on_device,
        mesh=mesh,
        in_specs=(
            P("serve", "tensor"),
            P("serve", "tensor", None),
            P("serve"),
            P("serve"),
            P(None, "tensor"),
        ),
        out_specs=P("serve", "tensor"),
        check_vma=False,
    )
```
